32 devices in a mesh: grp: 2 (over y), gx: 4 (over z), gy: 2 (over x), gz: 2 (over core).
Axes of the slice: x: 2, y: 2, z: 4, core: 2. Of those that a mesh axis runs over, the one named last changes fastest.
Arguments:
- feats: bfloat16 [16, 128, 48, 256], P(None, ('grp', 'gx'), 'gy', 'gz'), parts along dimension 1, may hold values from -6 to 6
- kernel: bfloat16 [27, 16, 16], replicated, may hold values from -0.3125 to 0.3125
- proj: float32 [16], replicated, may hold values from -1.5 to 1.5
- perm: float32 [128, 48, 256], P(('grp', 'gx'), 'gy', 'gz'), parts along dimension 0, may hold values from 0.1 to 1
- source: float32 [128, 48, 256], P(('grp', 'gx'), 'gy', 'gz'), parts along dimension 0, may hold values from -6 to 6
Outputs:
- residual: float32 [128, 48, 256], P(('grp', 'gx'), 'gy', 'gz'), parts along dimension 0
- kernel_grad: float32 [54, 16, 16], P('grp'), parts along dimension 0
- proj_grad: float32 [32], P('grp'), parts along dimension 0
- feats_grad: bfloat16 [16, 128, 48, 256], P(None, ('grp', 'gx'), 'gy', 'gz'), parts along dimension 1
The draws below stay inside these ranges and needn't reach their ends.
There are 2 independent parts, one for each index of `grp`. The reference program is written for one: setup_inputs(seed, part) draws one part's arguments, and reference() takes and returns one part's arrays. A program takes and returns all parts, laid end to end along the dimension named above; an argument that names none is the same for every part. Nothing has to cross between parts.
All inputs are finite; a program needn't handle non-finite values.
Results may differ from the reference program's by a relative error of at most 0.013.
Values may be sent and summed in bfloat16 or wider, within the bound.
No kernel may reach another device: no remote copies, remote signals or barrier semaphores. Data moves between devices by JAX's collectives and lax.ppermute only.
A program may use at most 128 MiB of HBM per device.

```python
import math
import jax
import jax.numpy as jnp
from jax import lax

C = 16
NX = 64
NY = 48
NZ = 256


def levels(rng, dims, pieces, low, high):
    def one(dim, shards_of):
        draws = jax.random.uniform(jax.random.fold_in(jax.random.fold_in(rng, 6), dim), (shards_of,), jnp.float32, low / len(pieces), high / len(pieces))
        return jnp.repeat(jnp.exp(draws), dims[dim] // shards_of).reshape((-1,) + (1,) * (len(dims) - dim - 1))

    level = one(*pieces[0])
    for cut in pieces[1:]:
        level = level * one(*cut)
    return level


def bell_draw(own_key, extent, scale, limit, split=(), held_as=jnp.bfloat16):
    values = jax.random.normal(own_key, extent, jnp.float32) * scale
    if len(split) > 0:
        values = levels(own_key, extent, split, -0.22, 0.18) * values
    return jnp.clip(values, min=-limit, max=limit).astype(held_as)


def setup_inputs(seed: int = 0, part: int = 0) -> dict:
    key_list = jax.random.split(jax.random.key(seed), 6)
    part_splits = jax.random.split(jax.random.fold_in(key_list[5], part), 6)
    return {
        "feats": bell_draw(part_splits[0], (C, NX, NY, NZ), 1.0, 6.0, ((1, 4), (2, 2), (3, 2))),
        "kernel": bell_draw(key_list[1], (27, C, C), (27 * C) ** -0.5, 0.3125),
        "proj": bell_draw(key_list[2], (C,), C ** -0.5, 1.5, (), jnp.float32),
        "perm": jnp.clip(jnp.exp(math.log(1.0) - 2.3025851 * jax.random.uniform(part_splits[3], (NX, NY, NZ), jnp.float32) ** levels(part_splits[3], (NX, NY, NZ), ((0, 4), (1, 2), (2, 2)), -0.2, 0.2)), 0.1, 1.0),
        "source": bell_draw(part_splits[4], (NX, NY, NZ), 1.0, 6.0, ((0, 4), (1, 2), (2, 2)), jnp.float32),
    }


def conv_layer(padded, kernel):
    channels = kernel.shape[1]
    weights = kernel.reshape(3, 3, 3, channels, channels).transpose(3, 4, 0, 1, 2)
    result = lax.conv_general_dilated(padded[None], weights, (1, 1, 1), 'VALID', dimension_numbers=('NCDHW', 'OIDHW', 'NCDHW'), precision=lax.Precision.HIGHEST)
    return result[0]

def neighbour(values, dim_index, offset):
    picked = [slice(1, -1), slice(1, -1), slice(1, -1)]
    picked[dim_index] = slice(1 + offset, values.shape[dim_index] - 1 + offset)
    return values[tuple(picked)]

def stencil(field_pad, perm_pad):
    centre = field_pad[1:-1, 1:-1, 1:-1]
    coefficient = perm_pad[1:-1, 1:-1, 1:-1]
    summed = jnp.zeros_like(centre)
    for dim_index in range(3):
        for offset in (-1, 1):
            near_perm = neighbour(perm_pad, dim_index, offset)
            face = 2.0 * coefficient * near_perm / (coefficient + near_perm)
            summed = summed + face * (centre - neighbour(field_pad, dim_index, offset))
    return summed

def reference(feats, kernel, proj, perm, source):
    padded = jnp.pad(feats.astype(jnp.float32), ((0, 0), (1, 1), (1, 1), (1, 1)))
    pre, pullback = jax.vjp(conv_layer, padded, kernel.astype(jnp.float32))
    activated = jax.nn.silu(pre)
    pressure = jnp.einsum('c,cxyz->xyz', proj, activated)
    perm_pad = jnp.pad(perm, 1, mode='edge')
    residual = stencil(jnp.pad(pressure, 1), perm_pad) - source
    adjoint = stencil(jnp.pad(residual, 1), perm_pad)
    proj_grad = jnp.einsum('cxyz,xyz->c', activated, adjoint)
    sigmoid_pre = jax.nn.sigmoid(pre)
    slope = sigmoid_pre * (1.0 + pre * (1.0 - sigmoid_pre))
    pre_grad = (adjoint[None] * proj[:, None, None, None] * slope).astype(jnp.bfloat16)
    padded_grad, kernel_grad = pullback(pre_grad.astype(jnp.float32))
    feats_grad = padded_grad[:, 1:-1, 1:-1, 1:-1].astype(jnp.bfloat16)
    return (residual, kernel_grad, proj_grad, feats_grad)
```

```python
import jax
import jax.numpy as jnp
from jax import lax
from jax.experimental import pallas as pl
from jax.experimental.pallas import tpu as pltpu
from jax.sharding import PartitionSpec as P

GROUP = ("gx", "gy", "gz")
HALO = 4
F32 = jnp.float32
BF16 = jnp.bfloat16


def routes(sizes, target):
    nx, ny, nz = sizes
    pairs = []
    for x in range(nx):
        for y in range(ny):
            for z in range(nz):
                tx, ty, tz = target(x, y, z)
                if 0 <= tx < nx and 0 <= ty < ny:
                    pairs.append(((x * ny + y) * nz + z, (tx * ny + ty) * nz + tz))
    return pairs


def pack_kernel(sides, flags, feats, perm, source, own, swap, near, far, *edges):
    half = flags[0]
    channels, planes, rows, lanes = feats.shape
    count = channels * rows
    row_id = lax.broadcasted_iota(jnp.int32, (count, count), 0)
    col_id = lax.broadcasted_iota(jnp.int32, (count, count), 1)
    order = (row_id % channels) * rows + row_id // channels
    permute = jnp.where(order == col_id, 1.0, 0.0).astype(BF16)
    wide = planes * 3 // 4

    def put(ref, index, limit, value):
        @pl.when((index >= 0) & (index < limit))
        def _():
            ref[index] = value

    def pair_step(pair, carry):
        x0 = pair * 2
        parts = [feats[:, x0 + j].astype(F32).reshape(count, lanes).astype(BF16) for j in range(2)]
        moved = jnp.dot(permute, jnp.concatenate(parts, axis=1), preferred_element_type=F32)
        for j in range(2):
            x = x0 + j
            cells = moved[:, j * lanes : (j + 1) * lanes]
            coefficient = perm[x]
            term = source[x]
            coefficient_hi = coefficient.astype(BF16).astype(F32)
            term_hi = term.astype(BF16).astype(F32)
            extra = [coefficient_hi, coefficient - coefficient_hi, term_hi, term - term_hi]
            plane = jnp.concatenate([cells] + extra, axis=0).astype(BF16)
            own[x] = plane
            put(swap, x - HALO * (1 - half), wide, plane)
            high = x - (planes - HALO)
            put(near, jnp.where(half == 0, high, x), HALO, plane)
            put(far, jnp.where(half == 0, x, high), HALO, plane)
            pieces = []
            for low_side in (True, False):
                start = 0 if low_side else rows - HALO
                pieces.append(
                    jnp.concatenate(
                        [cells[start * channels : (start + HALO) * channels]]
                        + [e[start : start + HALO] for e in extra],
                        axis=0,
                    )
                )
            if sides == 1:
                pieces = [jnp.where(flags[1] == 0, pieces[1], pieces[0])]
            else:
                pieces = [pieces[1], pieces[0]]
            for side in range(sides):
                piece = pieces[side].astype(BF16)
                e_same, e_cross, e_near, e_far = edges[4 * side : 4 * side + 4]
                put(e_same, x - HALO * half, wide, piece)
                put(e_cross, x - HALO * (1 - half), wide, piece)
                put(e_near, jnp.where(half == 0, high, x), HALO, piece)
                put(e_far, jnp.where(half == 0, x, high), HALO, piece)
        return carry

    lax.fori_loop(0, planes // 2, pair_step, 0)


def pack(feats, perm, source, flags, sides):
    channels, planes, rows, lanes = feats.shape
    full = rows * (channels + 4)
    edge = HALO * (channels + 4)
    wide = planes * 3 // 4
    shapes = [(planes, full), (wide, full), (HALO, full), (HALO, full)]
    shapes += [(wide, edge), (wide, edge), (HALO, edge), (HALO, edge)] * sides
    return pl.pallas_call(
        lambda *refs: pack_kernel(sides, *refs),
        out_shape=[jax.ShapeDtypeStruct(s + (lanes,), BF16) for s in shapes],
        in_specs=[pl.BlockSpec(memory_space=pltpu.SMEM)] + [pl.BlockSpec(memory_space=pltpu.VMEM)] * 3,
        out_specs=[pl.BlockSpec(memory_space=pltpu.VMEM)] * len(shapes),
        name="pack",
    )(flags, feats, perm, source)


def lane_shift(value, offset):
    size = value.shape[1]
    lane = lax.broadcasted_iota(jnp.int32, value.shape, 1)
    if offset < 0:
        return jnp.where(lane == 0, 0.0, pltpu.roll(value, 1, 1))
    return jnp.where(lane == size - 1, 0.0, pltpu.roll(value, size - 1, 1))


def sigmoid(value):
    return 0.5 * jnp.tanh(0.5 * value) + 0.5


def main_kernel(
    channels, rows, flags,
    own, swap, near, far, lo_same, lo_cross, lo_near, lo_far, hi_same, hi_cross, hi_near, hi_far,
    weights_fwd, weights_bwd, proj_rows,
    res_own, res_send, fg_own, fg_send, grads,
    fwide, gwide, pre_ref, coef, src, vfield, face_x, face_y, face_z, rfield, afield,
    acc_a, acc_b, kacc, pacc,
):
    half, has_ylo, has_yhi, has_xlo, has_xhi = (flags[i] for i in (0, 2, 3, 4, 5))
    lanes = own.shape[2]
    zsize = 2 * lanes
    ext_y = rows + 2 * HALO
    wide = swap.shape[0]
    ext_x = wide + HALO
    inner = ext_x - 2 * HALO
    taps = 3 * channels
    window = 10 * taps
    block = 8 * channels
    yblocks = ext_y // 8
    oblocks = rows // 8
    cell_rows = rows * channels
    edge_rows = HALO * channels

    def spread(ref, index, value, y0):
        n = value.shape[0] // channels
        for tap, shifted in enumerate((lane_shift(value, -1), value, lane_shift(value, 1))):
            for side in range(2):
                piece = shifted[:, side * lanes : (side + 1) * lanes].astype(BF16)
                ref[index, side, pl.ds(y0, n), tap * channels : (tap + 1) * channels, :] = piece.reshape(
                    n, channels, lanes
                )

    def joined(mine, other):
        a = mine.astype(F32)
        b = other.astype(F32)
        return jnp.concatenate([jnp.where(half == 0, a, b), jnp.where(half == 0, b, a)], axis=1)

    def fill(e, main_mine, main_other, lo_mine, lo_other, hi_mine, hi_other):
        centre = joined(main_mine, main_other)
        low = joined(lo_mine, lo_other)
        high = joined(hi_mine, hi_other)
        spread(fwide, e, jnp.where(has_ylo == 1, low[:edge_rows], 0.0), 1)
        spread(fwide, e, centre[:cell_rows], 1 + HALO)
        spread(fwide, e, jnp.where(has_yhi == 1, high[:edge_rows], 0.0), 1 + HALO + rows)
        zero = jnp.zeros((1, taps, lanes), BF16)
        for side in range(2):
            fwide[e, side, 0:1] = zero
            fwide[e, side, ext_y + 1 : ext_y + 2] = zero

        def full(kind):
            def at(value, base, n):
                start = base + kind * n
                return value[start : start + n] + value[start + n : start + 2 * n]

            mid = at(centre, cell_rows, rows)
            first = jnp.where(has_ylo == 1, at(low, edge_rows, HALO), mid[0:1])
            last = jnp.where(has_yhi == 1, at(high, edge_rows, HALO), mid[rows - 1 : rows])
            return jnp.concatenate([first, mid, last], axis=0)

        coef[e] = full(0)
        src[e] = full(2)

    def fill_wide(j, carry):
        fill(j + HALO * (1 - half), own[HALO * half + j], swap[j], lo_same[j], lo_cross[j], hi_same[j], hi_cross[j])
        return carry

    lax.fori_loop(0, wide, fill_wide, 0)

    def fill_far(j, carry):
        fill(j + wide * half, near[j], far[j], lo_near[j], lo_far[j], hi_near[j], hi_far[j])
        return carry

    lax.fori_loop(0, HALO, fill_far, 0)

    @pl.when(has_xlo == 0)
    def _():
        for e in range(HALO):
            coef[e] = coef[HALO]

    @pl.when(has_xhi == 0)
    def _():
        for e in range(ext_x - HALO, ext_x):
            coef[e] = coef[ext_x - HALO - 1]

    proj_block = jnp.concatenate([proj_rows[...]] * 8, axis=0)
    row_index = lax.broadcasted_iota(jnp.int32, (ext_y, zsize), 0)
    y_inside = ((row_index >= HALO) | (has_ylo == 1)) & ((row_index < HALO + rows) | (has_yhi == 1))
    lane_index = lax.broadcasted_iota(jnp.int32, (ext_y, zsize), 1)

    def masked(e, value):
        x_inside = ((e >= HALO) | (has_xlo == 1)) & ((e < ext_x - HALO) | (has_xhi == 1))
        return jnp.where(y_inside & x_inside, value, 0.0)

    def taps_of(ref, e, y0):
        return jnp.concatenate([ref[e, s, pl.ds(y0, 10)].reshape(window, lanes) for s in range(2)], axis=1)

    for yb in range(yblocks):

        def product(e):
            return jnp.dot(weights_fwd[...], taps_of(fwide, e, 8 * yb), preferred_element_type=F32)

        first = product(0)
        second = product(1)
        acc_b[0] = first[:block] + second[block : 2 * block]
        acc_a[0] = second[:block]

        def conv_step(e, carry):
            result = product(e)
            pre = acc_b[0] + result[2 * block :]
            acc_b[0] = acc_a[0] + result[block : 2 * block]
            acc_a[0] = result[:block]
            pre_ref[e - 2, yb] = pre
            active = pre * sigmoid(pre) * proj_block
            vfield[e - 2, 8 * yb : 8 * yb + 8, :] = jnp.sum(active.reshape(8, channels, zsize), axis=1)
            return carry

        lax.fori_loop(2, ext_x, conv_step, 0)

    def face(a, b):
        return 2.0 * a * b / (a + b)

    def face_step(e, carry):
        centre = coef[e]
        face_x[e] = face(centre, coef[jnp.minimum(e + 1, ext_x - 1)])
        face_y[e] = face(centre, pltpu.roll(centre, ext_y - 1, 0))
        face_z[e] = jnp.where(lane_index == zsize - 1, centre, face(centre, pltpu.roll(centre, zsize - 1, 1)))
        return carry

    lax.fori_loop(0, ext_x, face_step, 0)

    def operator(e, below, centre, above):
        flux_y = face_y[e] * (centre - pltpu.roll(centre, ext_y - 1, 0))
        flux_z = face_z[e] * (centre - lane_shift(centre, 1))
        left_z = jnp.where(lane_index == 0, -coef[e] * centre, pltpu.roll(flux_z, 1, 1))
        total = face_x[e] * (centre - above) + face_x[e - 1] * (centre - below)
        return total + (flux_y - pltpu.roll(flux_y, 1, 0)) + (flux_z - left_z)

    def mask_step(i, carry):
        vfield[i] = masked(i + 1, vfield[i])
        return carry

    lax.fori_loop(0, ext_x - 2, mask_step, 0)

    def residual_step(i, carry):
        value = operator(i + 2, vfield[i], vfield[i + 1], vfield[i + 2]) - src[i + 2]
        rfield[i] = masked(i + 2, value)
        return carry

    lax.fori_loop(0, ext_x - 4, residual_step, 0)

    def residual_out(x, carry):
        value = rfield[x + 2][HALO : HALO + rows]
        low = value[:, :lanes]
        high = value[:, lanes:]
        res_own[x] = jnp.where(half == 0, low, high)
        res_send[x] = jnp.where(half == 0, high, low)
        return carry

    lax.fori_loop(0, inner, residual_out, 0)

    def adjoint_step(i, carry):
        afield[i] = masked(i + 3, operator(i + 3, rfield[i], rfield[i + 1], rfield[i + 2]))
        return carry

    lax.fori_loop(0, ext_x - 6, adjoint_step, 0)

    pacc[...] = jnp.zeros(pacc.shape, F32)

    def grad_step(i, carry):
        for yb in range(yblocks):
            pre = pre_ref[i + 2, yb]
            sig = sigmoid(pre)
            near_adj = afield[i, 8 * yb : 8 * yb + 8, :]
            adj = jnp.broadcast_to(near_adj[:, None, :], (8, channels, zsize)).reshape(block, zsize)
            slope = sig * (1.0 + pre * (1.0 - sig))
            value = (adj * proj_block * slope).astype(BF16).astype(F32)
            spread(gwide, i, value, 8 * yb + 1)
            lo = max(HALO - 8 * yb, 0)
            hi = min(HALO + rows - 8 * yb, 8)
            term = (adj * (pre * sig))[lo * channels : hi * channels]
            total = term[:channels]
            for y in range(1, hi - lo):
                total = total + term[y * channels : (y + 1) * channels]

            @pl.when((i >= 1) & (i <= inner))
            def _():
                pacc[...] += total

        return carry

    lax.fori_loop(0, ext_x - 6, grad_step, 0)

    def back_product(i, b):
        return jnp.dot(weights_bwd[...], taps_of(gwide, i, HALO + 8 * b), preferred_element_type=F32)

    for b in range(oblocks):
        first = back_product(0, b)
        second = back_product(1, b)
        acc_b[b] = first[:block] + second[block : 2 * block]
        acc_a[b] = second[:block]

    def back_step(i, carry):
        parts = []
        for b in range(oblocks):
            result = back_product(i, b)
            parts.append((acc_b[b] + result[2 * block :]).reshape(channels, 8, zsize))
            acc_b[b] = acc_a[b] + result[block : 2 * block]
            acc_a[b] = result[:block]
        value = jnp.concatenate(parts, axis=1)
        low = value[:, :, :lanes]
        high = value[:, :, lanes:]
        fg_own[:, i - 2] = jnp.where(half == 0, low, high).astype(BF16)
        fg_send[:, i - 2] = jnp.where(half == 0, high, low).astype(BF16)
        return carry

    lax.fori_loop(2, inner + 2, back_step, 0)

    kacc[...] = jnp.zeros(kacc.shape, F32)

    def kernel_step(x, carry):
        for dx in range(3):
            total = kacc[dx]
            for b in range(oblocks):
                y0 = HALO + 1 + 8 * b
                pieces = [
                    gwide[x + 1, s, y0 : y0 + 8, channels : 2 * channels, :].reshape(block, lanes) for s in range(2)
                ]
                total = total + lax.dot_general(
                    taps_of(fwide, x + HALO - 1 + dx, HALO + 8 * b),
                    jnp.concatenate(pieces, axis=1),
                    (((1,), (1,)), ((), ())),
                    preferred_element_type=F32,
                )
            kacc[dx] = total
        return carry

    lax.fori_loop(0, inner, kernel_step, 0)

    lane_group = lax.broadcasted_iota(jnp.int32, (3 * taps, block), 1) // channels
    sub_row = lax.broadcasted_iota(jnp.int32, (3 * taps, block), 0) % (block // channels)
    per_dx = 3 * taps * channels // block
    for dx in range(3):
        picked = jnp.zeros((3 * taps, block), F32)
        for y in range(8):
            picked = jnp.where(lane_group == y, kacc[dx, y * taps : y * taps + 3 * taps], picked)
        step = channels
        while step < block:
            picked = picked + pltpu.roll(picked, step, 1)
            step *= 2
        packed = jnp.where(lane_group == sub_row, picked, 0.0).reshape(per_dx, block // channels, block)
        grads[dx * per_dx : (dx + 1) * per_dx, :] = jnp.sum(packed, axis=1)
    per_channel = jnp.sum(pacc[...], axis=1, keepdims=True)
    chan_row = lax.broadcasted_iota(jnp.int32, (channels, block), 0)
    chan_lane = lax.broadcasted_iota(jnp.int32, (channels, block), 1)
    flat = jnp.sum(jnp.where(chan_row == chan_lane, per_channel, 0.0), axis=0, keepdims=True)
    grads[3 * per_dx :, :] = jnp.broadcast_to(flat, (grads.shape[0] - 3 * per_dx, block))


def main(channels, rows, flags, tensors, weights_fwd, weights_bwd, proj_rows):
    own, swap = tensors[0], tensors[1]
    lanes = own.shape[2]
    zsize = 2 * lanes
    wide = swap.shape[0]
    ext_x = wide + HALO
    ext_y = rows + 2 * HALO
    inner = ext_x - 2 * HALO
    taps = 3 * channels
    block = 8 * channels
    oblocks = rows // 8
    grad_rows = 27 * channels * channels // block
    out_rows = -(-(grad_rows + 1) // 8) * 8
    vmem = pl.BlockSpec(memory_space=pltpu.VMEM)
    plane = (ext_y, zsize)
    return pl.pallas_call(
        lambda *refs: main_kernel(channels, rows, *refs),
        out_shape=[
            jax.ShapeDtypeStruct((inner, rows, lanes), F32),
            jax.ShapeDtypeStruct((inner, rows, lanes), F32),
            jax.ShapeDtypeStruct((channels, inner, rows, lanes), BF16),
            jax.ShapeDtypeStruct((channels, inner, rows, lanes), BF16),
            jax.ShapeDtypeStruct((out_rows, block), F32),
        ],
        in_specs=[pl.BlockSpec(memory_space=pltpu.SMEM)] + [vmem] * (len(tensors) + 3),
        out_specs=[vmem] * 5,
        scratch_shapes=[
            pltpu.VMEM((ext_x, 2, ext_y + 2, taps, lanes), BF16),
            pltpu.VMEM((ext_x - 6, 2, ext_y + 2, taps, lanes), BF16),
            pltpu.VMEM((ext_x - 2, ext_y // 8, block, zsize), F32),
            pltpu.VMEM((ext_x,) + plane, F32),
            pltpu.VMEM((ext_x,) + plane, F32),
            pltpu.VMEM((ext_x - 2,) + plane, F32),
            pltpu.VMEM((ext_x,) + plane, F32),
            pltpu.VMEM((ext_x,) + plane, F32),
            pltpu.VMEM((ext_x,) + plane, F32),
            pltpu.VMEM((ext_x - 4,) + plane, F32),
            pltpu.VMEM((ext_x - 6,) + plane, F32),
            pltpu.VMEM((oblocks, block, zsize), F32),
            pltpu.VMEM((oblocks, block, zsize), F32),
            pltpu.VMEM((3, 10 * taps, block), F32),
            pltpu.VMEM((channels, zsize), F32),
        ],
        compiler_params=pltpu.CompilerParams(vmem_limit_bytes=58 * 1024 * 1024),
        name="step",
    )(flags, *tensors, weights_fwd, weights_bwd, proj_rows)


def band(base, y):
    rest = 7 * base.shape[-1] // 3
    shift = y * base.shape[-1] // 3
    return jnp.pad(base, ((0, 0), (0, 0), (shift, rest - shift)))


def banded_weights(kernel):
    channels = kernel.shape[1]
    grid = kernel.reshape(3, 9, channels, channels)
    base = grid.transpose(0, 2, 1, 3).reshape(3, channels, 9 * channels)
    forward = jnp.stack([band(base, y) for y in range(8)], axis=1)
    flipped = grid[::-1, ::-1].transpose(0, 3, 1, 2).reshape(3, channels, 9 * channels)
    backward = jnp.stack([band(flipped, y) for y in range(8)], axis=2)
    return forward.reshape(24 * channels, -1), backward.reshape(24 * channels, -1)


def local(feats, kernel, proj, perm, source):
    channels, planes, rows, lanes = feats.shape
    sizes = tuple(lax.axis_size(a) for a in GROUP)
    nx, ny, _ = sizes
    gx, gy, half = (lax.axis_index(a) for a in GROUP)
    has_xlo = (gx > 0) | (half == 1)
    has_xhi = (gx < nx - 1) | (half == 0)
    flags = jnp.stack([half, gy, gy > 0, gy < ny - 1, has_xlo, has_xhi]).astype(jnp.int32)
    sides = 1 if ny == 2 else 2

    def send(value, target):
        return lax.ppermute(value, GROUP, routes(sizes, target))

    def step_x(x, z):
        return x + 1 if z == 0 else x - 1

    def step_far(x, z):
        return x - 1 if z == 0 else x + 1

    own, swap, near, far, *edges = pack(feats, perm, source, flags, sides)
    got = [own]
    got.append(send(swap, lambda x, y, z: (x, y, 1 - z)))
    got.append(send(near, lambda x, y, z: (step_x(x, z), y, z)))
    got.append(send(far, lambda x, y, z: (step_far(x, z), y, 1 - z)))
    received = []
    for side in range(sides):
        same, cross, e_near, e_far = edges[4 * side : 4 * side + 4]

        def step_y(y, side=side):
            if sides == 1:
                return 1 - y
            return y + 1 if side == 0 else y - 1

        received.append(
            [
                send(same, lambda x, y, z: (x, step_y(y), z)),
                send(cross, lambda x, y, z: (x, step_y(y), 1 - z)),
                send(e_near, lambda x, y, z: (step_x(x, z), step_y(y), z)),
                send(e_far, lambda x, y, z: (step_far(x, z), step_y(y), 1 - z)),
            ]
        )
    got += received[0] + received[-1]
    weights_fwd, weights_bwd = banded_weights(kernel)
    proj_rows = jnp.broadcast_to(proj[:, None], (channels, 2 * lanes))
    res_own, res_send, fg_own, fg_send, grads = main(
        channels, rows, flags, got, weights_fwd, weights_bwd, proj_rows
    )

    def partner(value):
        return send(value, lambda x, y, z: (x, y, 1 - z))

    res_got = partner(res_send)
    fg_got = partner(fg_send)

    def ordered(mine, other, axis):
        return jnp.where(
            half == 0, jnp.concatenate([mine, other], axis), jnp.concatenate([other, mine], axis)
        )

    residual = ordered(res_own, res_got, 0)
    feats_grad = ordered(fg_own, fg_got, 1)
    grads = grads + partner(grads)
    for axis in ("gy", "gx"):
        count = lax.axis_size(axis)
        step = 1
        while step < count:
            grads = grads + lax.ppermute(grads, axis, [(i, i ^ step) for i in range(count)])
            step *= 2
    grad_rows = 27 * channels * channels // grads.shape[1]
    kernel_grad = grads[:grad_rows].reshape(27, channels, channels).transpose(0, 2, 1)
    proj_grad = grads[grad_rows, :channels]
    return (residual, kernel_grad, proj_grad, feats_grad)


def solution(mesh):
    in_specs = (
        P(None, ("grp", "gx"), "gy", "gz"),
        P(),
        P(),
        P(("grp", "gx"), "gy", "gz"),
        P(("grp", "gx"), "gy", "gz"),
    )
    out_specs = (
        P(("grp", "gx"), "gy", "gz"),
        P("grp", None, None),
        P("grp"),
        P(None, ("grp", "gx"), "gy", "gz"),
    )
    return jax.shard_map(local, mesh=mesh, in_specs=in_specs, out_specs=out_specs, check_vma=False)
```

```python
import jax
import jax.numpy as jnp
from jax import lax
from jax.experimental import pallas as pl
from jax.experimental.pallas import tpu as pltpu
from jax.sharding import PartitionSpec as P

GROUP = ("gx", "gy", "gz")
HALO = 4
F32 = jnp.float32
BF16 = jnp.bfloat16


def routes(sizes, target):
    nx, ny, nz = sizes
    pairs = []
    for x in range(nx):
        for y in range(ny):
            for z in range(nz):
                tx, ty, tz = target(x, y, z)
                if 0 <= tx < nx and 0 <= ty < ny:
                    pairs.append(((x * ny + y) * nz + z, (tx * ny + ty) * nz + tz))
    return pairs


def pack_kernel(sides, feats, perm, source, own, swap, near, far, *edges):
    half = lax.axis_index("gz")
    at_y = lax.axis_index("gy")
    channels, planes, rows, lanes = feats.shape
    count = channels * rows
    row_id = lax.broadcasted_iota(jnp.int32, (count, count), 0)
    col_id = lax.broadcasted_iota(jnp.int32, (count, count), 1)
    order = (row_id % channels) * rows + row_id // channels
    permute = jnp.where(order == col_id, 1.0, 0.0).astype(BF16)
    wide = planes - HALO

    def put(ref, index, limit, value):
        @pl.when((index >= 0) & (index < limit))
        def _():
            ref[index] = value

    def pair_step(pair, carry):
        x0 = pair * 2
        parts = [feats[:, x0 + j].astype(F32).reshape(count, lanes).astype(BF16) for j in range(2)]
        moved = jnp.dot(permute, jnp.concatenate(parts, axis=1), preferred_element_type=F32)
        for j in range(2):
            x = x0 + j
            cells = moved[:, j * lanes : (j + 1) * lanes]
            coefficient = perm[x]
            term = source[x]
            coefficient_hi = coefficient.astype(BF16).astype(F32)
            term_hi = term.astype(BF16).astype(F32)
            extra = [coefficient_hi, coefficient - coefficient_hi, term_hi, term - term_hi]
            plane = jnp.concatenate([cells] + extra, axis=0).astype(BF16)
            own[x] = plane
            put(swap, x - HALO * (1 - half), wide, plane)
            high = x - wide
            put(near, jnp.where(half == 0, high, x), HALO, plane)
            put(far, jnp.where(half == 0, x, high), HALO, plane)
            pieces = []
            for start in (rows - HALO, 0):
                lines = [cells[start * channels : (start + HALO) * channels]]
                pieces.append(jnp.concatenate(lines + [e[start : start + HALO] for e in extra], axis=0))
            if sides == 1:
                pieces = [jnp.where(at_y == 0, pieces[0], pieces[1])]
            for side in range(sides):
                edges[side][x] = pieces[side].astype(BF16)
        return carry

    lax.fori_loop(0, planes // 2, pair_step, 0)


def pack(feats, perm, source, sides):
    channels, planes, rows, lanes = feats.shape
    full = rows * (channels + 4)
    edge = HALO * (channels + 4)
    shapes = [(planes, full), (planes - HALO, full), (HALO, full), (HALO, full)] + [(planes, edge)] * sides
    vmem = pl.BlockSpec(memory_space=pltpu.VMEM)
    return pl.pallas_call(
        lambda *refs: pack_kernel(sides, *refs),
        out_shape=[jax.ShapeDtypeStruct(s + (lanes,), BF16) for s in shapes],
        in_specs=[vmem] * 3,
        out_specs=[vmem] * len(shapes),
        name="pack",
    )(feats, perm, source)


def weights_kernel(base, forward, backward):
    channels = base.shape[2]
    taps = 3 * channels
    block = 8 * channels
    width = forward.shape[1]
    size = -(-width // 128) * 128
    blank = jnp.zeros((channels, size - 3 * taps), F32)
    place = lax.broadcasted_iota(jnp.int32, (block, size), 0) % 8
    for dx in range(3):
        line = jnp.concatenate([base[0, dx].astype(F32), blank], axis=1)
        for y in range(8):
            moved = line if y == 0 else pltpu.roll(line, y * taps, 1)
            start = dx * block + y * channels
            forward[start : start + channels, :] = moved[:, :width].astype(BF16)
        line = jnp.concatenate([base[1, dx].astype(F32), blank], axis=1)
        lines = jnp.broadcast_to(line[:, None, :], (channels, 8, size)).reshape(block, size)
        out = lines
        for y in range(1, 8):
            out = jnp.where(place == y, pltpu.roll(lines, y * taps, 1), out)
        backward[dx * block : (dx + 1) * block, :] = out[:, :width].astype(BF16)


def banded_weights(kernel):
    channels = kernel.shape[1]
    grid = kernel.reshape(3, 9, channels, channels)
    base = grid.transpose(0, 2, 1, 3).reshape(3, channels, 9 * channels)
    flipped = grid[::-1, ::-1].transpose(0, 3, 1, 2).reshape(3, channels, 9 * channels)
    vmem = pl.BlockSpec(memory_space=pltpu.VMEM)
    shape = jax.ShapeDtypeStruct((24 * channels, 30 * channels), BF16)
    return pl.pallas_call(
        weights_kernel, out_shape=[shape, shape], in_specs=[vmem], out_specs=[vmem, vmem], name="weights"
    )(jnp.stack([base, flipped]))


def sigmoid(value):
    return 0.5 * jnp.tanh(0.5 * value) + 0.5


def main_kernel(channels, rows, sides, proj, weights_fwd, weights_bwd, own, swap, near, far, *rest):
    edges = rest[: 4 * sides]
    (
        res_own, res_send, fg_own, fg_send, grads,
        raw_mine, raw_other, edge_mine, edge_other, sems,
        fwide, slot_a, slot_b, pre_ref, coef, src, vfield, face_x, face_y, face_z, rfield, afield,
        acc_a, acc_b, kacc, pacc,
    ) = rest[4 * sides :]
    half = lax.axis_index("gz")
    at_x = lax.axis_index("gx")
    at_y = lax.axis_index("gy")
    has_xlo = (at_x > 0) | (half == 1)
    has_xhi = (at_x < lax.axis_size("gx") - 1) | (half == 0)
    has_ylo = at_y > 0
    has_yhi = at_y < lax.axis_size("gy") - 1
    lanes = own.shape[2]
    zsize = 2 * lanes
    ext_y = rows + 2 * HALO
    wide = swap.shape[0]
    ext_x = wide + HALO
    inner = ext_x - 2 * HALO
    taps = 3 * channels
    window = 10 * taps
    block = 8 * channels
    yblocks = ext_y // 8
    oblocks = rows // 8
    cell_rows = rows * channels
    edge_rows = HALO * channels

    most = pl.ds(HALO * (1 - half), wide)
    side_part = pl.ds(wide * half, HALO)
    held = pl.ds(HALO * half, wide)
    moves = [
        (own.at[held], raw_mine.at[most]),
        (near, raw_mine.at[side_part]),
        (swap, raw_other.at[most]),
        (far, raw_other.at[side_part]),
    ]
    for s in range(sides):
        e_own, e_swap, e_near, e_far = edges[4 * s : 4 * s + 4]
        moves += [
            (e_own.at[held], edge_mine.at[s, most]),
            (e_near, edge_mine.at[s, side_part]),
            (e_swap.at[held], edge_other.at[s, most]),
            (e_far, edge_other.at[s, side_part]),
        ]
    copies = [pltpu.make_async_copy(a, b, sems.at[k]) for k, (a, b) in enumerate(moves)]
    for copy in copies:
        copy.start()

    lane_row = lax.broadcasted_iota(jnp.int32, (1, zsize), 1)
    not_first = jnp.where(lane_row == 0, 0.0, 1.0).astype(BF16)
    not_last = jnp.where(lane_row == zsize - 1, 0.0, 1.0).astype(BF16)
    sub = lax.broadcasted_iota(jnp.int32, (channels, zsize), 0)
    proj_rows = jnp.zeros((channels, zsize), F32)
    tile_lane = lax.broadcasted_iota(jnp.int32, (16, 2 * block), 1) % block
    tile_row = lax.broadcasted_iota(jnp.int32, (16, 2 * block), 0)
    tile_low = lax.broadcasted_iota(jnp.int32, (16, 2 * block), 1) < block
    proj_lanes = jnp.zeros((16, 2 * block), F32)
    for c in range(channels):
        proj_rows = jnp.where(sub == c, proj[c], proj_rows)
        proj_lanes = jnp.where(tile_lane % channels == c, proj[c], proj_lanes)
    proj_block = jnp.concatenate([proj_rows] * 8, axis=0)
    proj_hi = proj_lanes.astype(BF16).astype(F32)
    on_row = tile_lane // channels == tile_row % 8
    reduce_hi = jnp.where(on_row & (tile_row < 8), proj_hi, 0.0)
    reduce_lo = jnp.where(on_row & (tile_row >= 8) & tile_low, proj_lanes - proj_hi, 0.0)
    reducer = (reduce_hi + reduce_lo).astype(BF16)
    row_index = lax.broadcasted_iota(jnp.int32, (ext_y, zsize), 0)
    y_inside = ((row_index >= HALO) | has_ylo) & ((row_index < HALO + rows) | has_yhi)
    lane_index = lax.broadcasted_iota(jnp.int32, (ext_y, zsize), 1)
    zero = jnp.zeros((1, taps, lanes), BF16)
    for e in range(ext_x):
        for s in range(2):
            fwide[e, s, 0:1] = zero
            fwide[e, s, ext_y + 1 : ext_y + 2] = zero
    kacc[...] = jnp.zeros(kacc.shape, F32)
    pacc[...] = jnp.zeros(pacc.shape, F32)
    acc_a[...] = jnp.zeros(acc_a.shape, F32)
    acc_b[...] = jnp.zeros(acc_b.shape, F32)
    for copy in copies:
        copy.wait()

    def spread(ref, value, y0):
        n = value.shape[0] // channels
        below = pltpu.roll(value, 1, 1) * not_first
        above = pltpu.roll(value, zsize - 1, 1) * not_last
        for tap, shifted in enumerate((below, value, above)):
            for s in range(2):
                piece = shifted[:, s * lanes : (s + 1) * lanes].reshape(n, channels, lanes)
                ref[s, y0 : y0 + n, tap * channels : (tap + 1) * channels, :] = piece

    def joined(mine, other):
        return jnp.concatenate([jnp.where(half == 0, mine, other), jnp.where(half == 0, other, mine)], axis=1)

    def part(e, start, stop):
        return joined(raw_mine[e, start:stop], raw_other[e, start:stop])

    def edge_part(s, e, start, stop):
        return joined(edge_mine[s, e, start:stop], edge_other[s, e, start:stop])

    def face(a, b):
        return 2.0 * a * b / (a + b)

    def fill_cells(e, k):
        start = 8 * k - HALO
        lo = max(start, 0)
        hi = min(start + 8, rows)
        value = part(e, lo * channels, hi * channels)
        blank = jnp.zeros((edge_rows, zsize), BF16)
        if start < 0:
            value = jnp.concatenate([jnp.where(has_ylo, edge_part(0, e, 0, edge_rows), blank), value], axis=0)
        if start + 8 > rows:
            value = jnp.concatenate([value, jnp.where(has_yhi, edge_part(sides - 1, e, 0, edge_rows), blank)], axis=0)
        spread(fwide.at[e], value, 8 * k + 1)

    def fill_fields(e):
        centre = part(e, cell_rows, cell_rows + 4 * rows).astype(F32)
        low = edge_part(0, e, edge_rows, edge_rows + 4 * HALO).astype(F32)
        high = edge_part(sides - 1, e, edge_rows, edge_rows + 4 * HALO).astype(F32)

        def full(kind):
            def at(value, n):
                start = kind * n
                return value[start : start + n] + value[start + n : start + 2 * n]

            mid = at(centre, rows)
            first = jnp.where(has_ylo, at(low, HALO), mid[0:1])
            last = jnp.where(has_yhi, at(high, HALO), mid[rows - 1 : rows])
            return jnp.concatenate([first, mid, last], axis=0)

        plane = full(0)
        coef[e] = plane
        src[e] = full(2)
        face_y[e] = face(plane, pltpu.roll(plane, ext_y - 1, 0))
        face_z[e] = jnp.where(lane_index == zsize - 1, plane, face(plane, pltpu.roll(plane, zsize - 1, 1)))
        before = jnp.maximum(e - 1, 0)
        face_x[before] = face(coef[before], plane)

    def x_inside(e):
        return ((e >= HALO) | has_xlo) & ((e < ext_x - HALO) | has_xhi)

    def masked(e, value):
        return jnp.where(y_inside & x_inside(e), value, 0.0)

    def taps_of(ref, y0):
        return jnp.concatenate([ref[s, y0 : y0 + 10].reshape(window, lanes) for s in range(2)], axis=1)

    def convolve(e, yb):
        result = jnp.dot(weights_fwd[...], taps_of(fwide.at[e], 8 * yb), preferred_element_type=F32)
        pre_ref[jnp.maximum(e - 2, 0), yb] = acc_b[yb] + result[2 * block :]
        acc_b[yb] = acc_a[yb] + result[block : 2 * block]
        acc_a[yb] = result[:block]

    def activate(px, yb):
        pre = pre_ref[px, yb]
        active = pre * sigmoid(pre)
        high = active.astype(BF16)
        low = (active - high.astype(F32)).astype(BF16)
        sums = jnp.dot(reducer, jnp.concatenate([high, low], axis=0), preferred_element_type=F32)
        inside = y_inside[8 * yb : 8 * yb + 8] & x_inside(px + 1)
        vfield[px, 8 * yb : 8 * yb + 8, :] = jnp.where(inside, sums[:8] + sums[8:], 0.0)

    for k in range(yblocks):
        fill_cells(0, k)
    fill_fields(0)

    def conv_step(e, carry):
        for k in range(yblocks):
            activate(jnp.maximum(e - 4, 0), k)
            convolve(e - 1, k)
            fill_cells(e, k)
        fill_fields(e)
        return carry

    lax.fori_loop(1, ext_x, conv_step, 0)
    for k in range(yblocks):
        activate(ext_x - 4, k)
        convolve(ext_x - 1, k)
    for k in range(yblocks):
        activate(ext_x - 3, k)

    @pl.when(jnp.logical_not(has_xlo))
    def _():
        face_x[HALO - 1] = coef[HALO]

    @pl.when(jnp.logical_not(has_xhi))
    def _():
        face_x[ext_x - HALO - 1] = coef[ext_x - HALO - 1]

    def operator(e, below, centre, above):
        flux_y = face_y[e] * (centre - pltpu.roll(centre, ext_y - 1, 0))
        next_z = jnp.where(lane_index == zsize - 1, 0.0, pltpu.roll(centre, zsize - 1, 1))
        flux_z = face_z[e] * (centre - next_z)
        left_z = jnp.where(lane_index == 0, -coef[e] * centre, pltpu.roll(flux_z, 1, 1))
        total = face_x[e] * (centre - above) + face_x[e - 1] * (centre - below)
        return total + (flux_y - pltpu.roll(flux_y, 1, 0)) + (flux_z - left_z)

    def residual_step(i, carry):
        value = operator(i + 2, vfield[i], vfield[i + 1], vfield[i + 2]) - src[i + 2]
        rfield[i] = masked(i + 2, value)
        return carry

    lax.fori_loop(0, ext_x - 4, residual_step, 0, unroll=4)

    def adjoint_step(i, carry):
        afield[i] = masked(i + 3, operator(i + 3, rfield[i], rfield[i + 1], rfield[i + 2]))
        return carry

    lax.fori_loop(0, ext_x - 6, adjoint_step, 0, unroll=5)

    def residual_out(x, carry):
        value = rfield[x + 2][HALO : HALO + rows]
        low = value[:, :lanes]
        high = value[:, lanes:]
        res_own[x] = jnp.where(half == 0, low, high)
        res_send[x] = jnp.where(half == 0, high, low)
        return carry

    lax.fori_loop(0, inner, residual_out, 0, unroll=4)

    def grad_block(i, yb, slot):
        pre = pre_ref[i + 2, yb]
        sig = sigmoid(pre)
        near_adj = afield[i, 8 * yb : 8 * yb + 8, :]
        adj = jnp.broadcast_to(near_adj[:, None, :], (8, channels, zsize)).reshape(block, zsize)
        slope = sig * (1.0 + pre * (1.0 - sig))
        spread(slot, (adj * proj_block * slope).astype(BF16), 8 * yb + 1)
        lo = max(HALO - 8 * yb, 0)
        hi = min(HALO + rows - 8 * yb, 8)
        term = (adj * (pre * sig))[lo * channels : hi * channels]
        total = term[:channels]
        for y in range(1, hi - lo):
            total = total + term[y * channels : (y + 1) * channels]
        pacc[...] += jnp.where((i >= 1) & (i <= inner), total, 0.0)

    def back_product(b, slot, weights):
        return jnp.dot(weights, taps_of(slot, HALO + 8 * b), preferred_element_type=F32)

    def store_plane(x, parts):
        value = jnp.concatenate([p.reshape(channels, 8, zsize) for p in parts], axis=1).astype(BF16)
        low = value[:, :, :lanes]
        high = value[:, :, lanes:]
        fg_own[:, x] = jnp.where(half == 0, low, high)
        fg_send[:, x] = jnp.where(half == 0, high, low)

    def multiply(i, slot, make):
        parts = []
        centres = []
        for b in range(oblocks):
            y0 = HALO + 1 + 8 * b
            pieces = [slot[s, y0 : y0 + 8, channels : 2 * channels, :].reshape(block, lanes) for s in range(2)]
            centres.append(jnp.concatenate(pieces, axis=1))
        for k in range(max(3, oblocks, yblocks)):
            if k < oblocks:
                result = back_product(k, slot, weights_bwd[...])
                parts.append(acc_b[k] + result[2 * block :])
                acc_b[k] = acc_a[k] + result[block : 2 * block]
                acc_a[k] = result[:block]
            if k < 3:
                total = kacc[k]
                for b in range(oblocks):
                    total = total + lax.dot_general(
                        taps_of(fwide.at[i + HALO - 2 + k], HALO + 8 * b),
                        centres[b],
                        (((1,), (1,)), ((), ())),
                        preferred_element_type=F32,
                    )
                kacc[k] = total
            if k < yblocks:
                make(k)
        store_plane(jnp.maximum(i - 2, 0), parts)

    for k in range(yblocks):
        grad_block(0, k, slot_a)
    for b in range(oblocks):
        acc_a[b] = back_product(b, slot_a, weights_bwd[:block])
        acc_b[b] = jnp.zeros((block, zsize), F32)
    for k in range(yblocks):
        grad_block(1, k, slot_b)

    def grad_step(t, carry):
        odd = 2 * t - 1
        multiply(odd, slot_b, lambda k: grad_block(odd + 1, k, slot_a))
        multiply(odd + 1, slot_a, lambda k: grad_block(odd + 2, k, slot_b))
        return carry

    lax.fori_loop(1, inner // 2 + 1, grad_step, 0)
    store_plane(inner - 1, [acc_b[b] + back_product(b, slot_b, weights_bwd[2 * block :]) for b in range(oblocks)])

    lane_group = lax.broadcasted_iota(jnp.int32, (3 * taps, block), 1) // channels
    sub_row = lax.broadcasted_iota(jnp.int32, (3 * taps, block), 0) % (block // channels)
    per_dx = 3 * taps * channels // block
    for dx in range(3):
        picked = jnp.zeros((3 * taps, block), F32)
        for y in range(8):
            picked = jnp.where(lane_group == y, kacc[dx, y * taps : y * taps + 3 * taps], picked)
        step = channels
        while step < block:
            picked = picked + pltpu.roll(picked, step, 1)
            step *= 2
        packed = jnp.where(lane_group == sub_row, picked, 0.0).reshape(per_dx, block // channels, block)
        grads[dx * per_dx : (dx + 1) * per_dx, :] = jnp.sum(packed, axis=1)
    per_channel = jnp.sum(pacc[...], axis=1, keepdims=True)
    chan_row = lax.broadcasted_iota(jnp.int32, (channels, block), 0)
    chan_lane = lax.broadcasted_iota(jnp.int32, (channels, block), 1)
    flat = jnp.sum(jnp.where(chan_row == chan_lane, per_channel, 0.0), axis=0, keepdims=True)
    grads[3 * per_dx :, :] = jnp.broadcast_to(flat, (grads.shape[0] - 3 * per_dx, block))


def main(channels, rows, proj, weights, tensors, edges):
    own, swap = tensors[0], tensors[1]
    sides = len(edges) // 4
    lanes = own.shape[2]
    zsize = 2 * lanes
    wide = swap.shape[0]
    ext_x = wide + HALO
    ext_y = rows + 2 * HALO
    inner = ext_x - 2 * HALO
    taps = 3 * channels
    block = 8 * channels
    yblocks = ext_y // 8
    grad_rows = 27 * channels * channels // block
    out_rows = -(-(grad_rows + 1) // 8) * 8
    vmem = pl.BlockSpec(memory_space=pltpu.VMEM)
    anywhere = pl.BlockSpec(memory_space=pl.ANY)
    plane = (ext_y, zsize)
    slot = pltpu.VMEM((2, ext_y + 2, taps, lanes), BF16)
    return pl.pallas_call(
        lambda *refs: main_kernel(channels, rows, sides, *refs),
        out_shape=[
            jax.ShapeDtypeStruct((inner, rows, lanes), F32),
            jax.ShapeDtypeStruct((inner, rows, lanes), F32),
            jax.ShapeDtypeStruct((channels, inner, rows, lanes), BF16),
            jax.ShapeDtypeStruct((channels, inner, rows, lanes), BF16),
            jax.ShapeDtypeStruct((out_rows, block), F32),
        ],
        in_specs=[pl.BlockSpec(memory_space=pltpu.SMEM)] + [vmem] * 2 + [anywhere] * (len(tensors) + len(edges)),
        out_specs=[vmem] * 5,
        scratch_shapes=[
            pltpu.VMEM((ext_x,) + own.shape[1:], BF16),
            pltpu.VMEM((ext_x,) + own.shape[1:], BF16),
            pltpu.VMEM((sides, ext_x) + edges[0].shape[1:], BF16),
            pltpu.VMEM((sides, ext_x) + edges[0].shape[1:], BF16),
            pltpu.SemaphoreType.DMA((4 + 4 * sides,)),
            pltpu.VMEM((ext_x, 2, ext_y + 2, taps, lanes), BF16),
            slot,
            slot,
            pltpu.VMEM((ext_x - 2, yblocks, block, zsize), F32),
            pltpu.VMEM((ext_x,) + plane, F32),
            pltpu.VMEM((ext_x,) + plane, F32),
            pltpu.VMEM((ext_x - 2,) + plane, F32),
            pltpu.VMEM((ext_x,) + plane, F32),
            pltpu.VMEM((ext_x,) + plane, F32),
            pltpu.VMEM((ext_x,) + plane, F32),
            pltpu.VMEM((ext_x - 4,) + plane, F32),
            pltpu.VMEM((ext_x - 6,) + plane, F32),
            pltpu.VMEM((yblocks, block, zsize), F32),
            pltpu.VMEM((yblocks, block, zsize), F32),
            pltpu.VMEM((3, 10 * taps, block), F32),
            pltpu.VMEM((channels, zsize), F32),
        ],
        compiler_params=pltpu.CompilerParams(vmem_limit_bytes=58 * 1024 * 1024),
        name="step",
    )(proj, *weights, *tensors, *edges)


def local(feats, kernel, proj, perm, source):
    channels, planes, rows, lanes = feats.shape
    sizes = tuple(lax.axis_size(a) for a in GROUP)
    ny = sizes[1]
    half = lax.axis_index("gz")
    sides = 1 if ny == 2 else 2

    def send(value, target):
        return lax.ppermute(value, GROUP, routes(sizes, target))

    def partner(value):
        return send(value, lambda x, y, z: (x, y, 1 - z))

    def to_near(value):
        return send(value, lambda x, y, z: (x + 1 if z == 0 else x - 1, y, z))

    def to_far(value):
        return send(value, lambda x, y, z: (x - 1 if z == 0 else x + 1, y, 1 - z))

    own, swap, near, far, *edges = pack(feats, perm, source, sides)
    received = []
    for side in range(sides):

        def step_y(y, side=side):
            if sides == 1:
                return 1 - y
            return y + 1 if side == 0 else y - 1

        received.append(send(edges[side], lambda x, y, z: (x, step_y(y), z)))
    tensors = [own, partner(swap), to_near(near), to_far(far)]
    wide = planes - HALO
    got = []
    for value in received:
        got += [
            value,
            partner(value),
            to_near(lax.dynamic_slice_in_dim(value, wide * (1 - half), HALO, 0)),
            to_far(lax.dynamic_slice_in_dim(value, wide * half, HALO, 0)),
        ]
    weights = banded_weights(kernel)
    res_own, res_send, fg_own, fg_send, grads = main(channels, rows, proj, weights, tensors, got)

    res_got = partner(res_send)
    fg_got = partner(fg_send)

    def ordered(mine, other, axis):
        return jnp.where(
            half == 0, jnp.concatenate([mine, other], axis), jnp.concatenate([other, mine], axis)
        )

    residual = ordered(res_own, res_got, 0)
    feats_grad = ordered(fg_own, fg_got, 1)
    grads = grads + partner(grads)
    for axis in ("gy", "gx"):
        count = lax.axis_size(axis)
        step = 1
        while step < count:
            grads = grads + lax.ppermute(grads, axis, [(i, i ^ step) for i in range(count)])
            step *= 2
    grad_rows = 27 * channels * channels // grads.shape[1]
    kernel_grad = grads[:grad_rows].reshape(27, channels, channels).transpose(0, 2, 1)
    proj_grad = grads[grad_rows, :channels]
    return (residual, kernel_grad, proj_grad, feats_grad)


def solution(mesh):
    in_specs = (
        P(None, ("grp", "gx"), "gy", "gz"),
        P(),
        P(),
        P(("grp", "gx"), "gy", "gz"),
        P(("grp", "gx"), "gy", "gz"),
    )
    out_specs = (
        P(("grp", "gx"), "gy", "gz"),
        P("grp", None, None),
        P("grp"),
        P(None, ("grp", "gx"), "gy", "gz"),
    )
    return jax.shard_map(local, mesh=mesh, in_specs=in_specs, out_specs=out_specs, check_vma=False)
```

```python
import jax
import jax.numpy as jnp
from jax import lax
from jax.experimental import pallas as pl
from jax.experimental.pallas import tpu as pltpu
from jax.sharding import PartitionSpec as P

GROUP = ("gx", "gy", "gz")
HALO = 4
STRIP = 3
F32 = jnp.float32
BF16 = jnp.bfloat16


def routes(sizes, target):
    nx, ny, nz = sizes
    pairs = []
    for x in range(nx):
        for y in range(ny):
            for z in range(nz):
                tx, ty, tz = target(x, y, z)
                if 0 <= tx < nx and 0 <= ty < ny:
                    pairs.append(((x * ny + y) * nz + z, (tx * ny + ty) * nz + tz))
    return pairs


def pack_kernel(sides, feats, perm, source, own, swap, near, far, *edges):
    half = lax.axis_index("gz")
    at_y = lax.axis_index("gy")
    channels, planes, rows, lanes = feats.shape
    count = channels * rows
    row_id = lax.broadcasted_iota(jnp.int32, (count, count), 0)
    col_id = lax.broadcasted_iota(jnp.int32, (count, count), 1)
    order = (row_id % channels) * rows + row_id // channels
    permute = jnp.where(order == col_id, 1.0, 0.0).astype(BF16)
    wide = planes - HALO

    def put(ref, index, limit, value):
        @pl.when((index >= 0) & (index < limit))
        def _():
            ref[index] = value

    def pair_step(pair, carry):
        x0 = pair * 2
        parts = [feats[:, x0 + j].astype(F32).reshape(count, lanes).astype(BF16) for j in range(2)]
        moved = jnp.dot(permute, jnp.concatenate(parts, axis=1), preferred_element_type=F32)
        for j in range(2):
            x = x0 + j
            cells = moved[:, j * lanes : (j + 1) * lanes]
            coefficient = perm[x]
            term = source[x]
            coefficient_hi = coefficient.astype(BF16).astype(F32)
            term_hi = term.astype(BF16).astype(F32)
            extra = [coefficient_hi, coefficient - coefficient_hi, term_hi, term - term_hi]
            plane = jnp.concatenate([cells] + extra, axis=0).astype(BF16)
            own[x] = plane
            put(swap, x - HALO * (1 - half), wide, plane)
            high = x - wide
            put(near, jnp.where(half == 0, high, x), HALO, plane)
            put(far, jnp.where(half == 0, x, high), HALO, plane)
            pieces = []
            for start in (rows - HALO, 0):
                lines = [cells[start * channels : (start + HALO) * channels]]
                pieces.append(jnp.concatenate(lines + [e[start : start + HALO] for e in extra], axis=0))
            if sides == 1:
                pieces = [jnp.where(at_y == 0, pieces[0], pieces[1])]
            for side in range(sides):
                edges[side][x] = pieces[side].astype(BF16)
        return carry

    lax.fori_loop(0, planes // 2, pair_step, 0)


def pack(feats, perm, source, sides):
    channels, planes, rows, lanes = feats.shape
    full = rows * (channels + 4)
    edge = HALO * (channels + 4)
    shapes = [(planes, full), (planes - HALO, full), (HALO, full), (HALO, full)] + [(planes, edge)] * sides
    vmem = pl.BlockSpec(memory_space=pltpu.VMEM)
    return pl.pallas_call(
        lambda *refs: pack_kernel(sides, *refs),
        out_shape=[jax.ShapeDtypeStruct(s + (lanes,), BF16) for s in shapes],
        in_specs=[vmem] * 3,
        out_specs=[vmem] * len(shapes),
        compiler_params=pltpu.CompilerParams(vmem_limit_bytes=14 * 1024 * 1024),
        name="pack",
    )(feats, perm, source)


def weights_kernel(base, flipped, forward, backward):
    channels = base.shape[1]
    taps = 3 * channels
    block = 8 * channels
    width = backward.shape[1]
    size = -(-width // 128) * 128
    blank = jnp.zeros((channels, size - 3 * taps), F32)
    place = lax.broadcasted_iota(jnp.int32, (block, size), 0) % 8
    for dx in range(3):
        line = jnp.concatenate([base[dx].astype(F32), blank], axis=1)
        for y in range(STRIP):
            moved = line if y == 0 else pltpu.roll(line, y * taps, 1)
            start = (dx * STRIP + y) * channels
            forward[start : start + channels, :] = moved[:, : forward.shape[1]].astype(BF16)
        line = jnp.concatenate([flipped[dx].astype(F32), blank], axis=1)
        lines = jnp.broadcast_to(line[:, None, :], (channels, 8, size)).reshape(block, size)
        out = lines
        for y in range(1, 8):
            moved = pltpu.roll(line, y * taps, 1)
            lines = jnp.broadcast_to(moved[:, None, :], (channels, 8, size)).reshape(block, size)
            out = jnp.where(place == y, lines, out)
        backward[dx * block : (dx + 1) * block, :] = out[:, :width].astype(BF16)


def banded_weights(kernel):
    channels = kernel.shape[1]
    grid = kernel.reshape(3, 9, channels, channels)
    base = grid.transpose(0, 2, 1, 3).reshape(3, channels, 9 * channels)
    flipped = grid[::-1, ::-1].transpose(0, 3, 1, 2).reshape(3, channels, 9 * channels)
    vmem = pl.BlockSpec(memory_space=pltpu.VMEM)
    shapes = [
        jax.ShapeDtypeStruct((3 * STRIP * channels, 3 * (STRIP + 2) * channels), BF16),
        jax.ShapeDtypeStruct((24 * channels, 30 * channels), BF16),
    ]
    return pl.pallas_call(
        weights_kernel, out_shape=shapes, in_specs=[vmem] * 2, out_specs=[vmem] * 2,
        compiler_params=pltpu.CompilerParams(vmem_limit_bytes=8 * 1024 * 1024), name="weights",
    )(base, flipped)


def sigmoid(value):
    return 0.5 * jnp.tanh(0.5 * value) + 0.5


def main_kernel(channels, rows, sides, proj, weights_fwd, weights_bwd, own, swap, near, far, *rest):
    edges = rest[: 4 * sides]
    (
        res_own, res_send, fg_own, fg_send, grads,
        fwide, slot_a, slot_b, pre_ref, coef, src, vfield, face_x, face_y, face_z, rfield, afield,
        conv_a, conv_b, acc_a, acc_b, kacc, pacc,
    ) = rest[4 * sides :]
    half = lax.axis_index("gz")
    at_x = lax.axis_index("gx")
    at_y = lax.axis_index("gy")
    has_xlo = (at_x > 0) | (half == 1)
    has_xhi = (at_x < lax.axis_size("gx") - 1) | (half == 0)
    has_ylo = at_y > 0
    has_yhi = at_y < lax.axis_size("gy") - 1
    lanes = own.shape[2]
    zsize = 2 * lanes
    ext_y = rows + 2 * HALO
    wide = swap.shape[0]
    ext_x = wide + HALO
    inner = ext_x - 2 * HALO
    taps = 3 * channels
    block = 8 * channels
    yblocks = ext_y // 8
    strip = STRIP * channels
    strips = (ext_y - 2) // STRIP
    oblocks = rows // 8
    cell_rows = rows * channels
    edge_rows = HALO * channels

    lane_row = lax.broadcasted_iota(jnp.int32, (1, zsize), 1)
    not_first = jnp.where(lane_row == 0, 0.0, 1.0).astype(BF16)
    not_last = jnp.where(lane_row == zsize - 1, 0.0, 1.0).astype(BF16)
    sub = lax.broadcasted_iota(jnp.int32, (channels, zsize), 0)
    proj_rows = jnp.zeros((channels, zsize), F32)
    for c in range(channels):
        proj_rows = jnp.where(sub == c, proj[c], proj_rows)
    proj_block = jnp.concatenate([proj_rows] * 8, axis=0)
    row_index = lax.broadcasted_iota(jnp.int32, (ext_y, zsize), 0)
    y_inside = ((row_index >= HALO) | has_ylo) & ((row_index < HALO + rows) | has_yhi)
    lane_index = lax.broadcasted_iota(jnp.int32, (ext_y, zsize), 1)
    for px in range(ext_x - 2):
        pre_ref[px, :channels, :] = jnp.zeros((channels, zsize), F32)
        pre_ref[px, (ext_y - 1) * channels :, :] = jnp.zeros((channels, zsize), F32)
    kacc[...] = jnp.zeros(kacc.shape, F32)
    pacc[...] = jnp.zeros(pacc.shape, F32)
    conv_a[...] = jnp.zeros(conv_a.shape, F32)
    conv_b[...] = jnp.zeros(conv_b.shape, F32)

    def spread(ref, value, y0):
        n = value.shape[0] // channels
        below = pltpu.roll(value, 1, 1) * not_first
        above = pltpu.roll(value, zsize - 1, 1) * not_last
        for tap, shifted in enumerate((below, value, above)):
            for s in range(2):
                piece = shifted[:, s * lanes : (s + 1) * lanes].reshape(n, channels, lanes)
                ref[s, y0 : y0 + n, tap * channels : (tap + 1) * channels, :] = piece

    def joined(mine, other):
        return jnp.concatenate([jnp.where(half == 0, mine, other), jnp.where(half == 0, other, mine)], axis=1)

    def place(e):
        at = e - HALO * (1 - half)
        most = (at >= 0) & (at < wide)
        return most, jnp.clip(at, 0, wide - 1), jnp.clip(e - wide * half, 0, HALO - 1)

    def part(e, start, stop):
        most, at, beside = place(e)
        mine = jnp.where(most, own[at + HALO * half, start:stop], near[beside, start:stop])
        return joined(mine, jnp.where(most, swap[at, start:stop], far[beside, start:stop]))

    def edge_part(s, e, start, stop):
        e_own, e_swap, e_near, e_far = edges[4 * s : 4 * s + 4]
        most, at, beside = place(e)
        mine = jnp.where(most, e_own[at + HALO * half, start:stop], e_near[beside, start:stop])
        return joined(mine, jnp.where(most, e_swap[at + HALO * half, start:stop], e_far[beside, start:stop]))

    def face(a, b):
        return 2.0 * a * b / (a + b)

    def fill_cells(e, k):
        start = 8 * k - HALO
        lo = max(start, 0)
        hi = min(start + 8, rows)
        value = part(e, lo * channels, hi * channels)
        blank = jnp.zeros((edge_rows, zsize), BF16)
        if start < 0:
            value = jnp.concatenate([jnp.where(has_ylo, edge_part(0, e, 0, edge_rows), blank), value], axis=0)
        if start + 8 > rows:
            value = jnp.concatenate([value, jnp.where(has_yhi, edge_part(sides - 1, e, 0, edge_rows), blank)], axis=0)
        spread(fwide.at[e], value, 8 * k)

    def fill_fields(e):
        centre = part(e, cell_rows, cell_rows + 4 * rows).astype(F32)
        low = edge_part(0, e, edge_rows, edge_rows + 4 * HALO).astype(F32)
        high = edge_part(sides - 1, e, edge_rows, edge_rows + 4 * HALO).astype(F32)

        def full(kind):
            def at(value, n):
                start = kind * n
                return value[start : start + n] + value[start + n : start + 2 * n]

            mid = at(centre, rows)
            first = jnp.where(has_ylo, at(low, HALO), mid[0:1])
            last = jnp.where(has_yhi, at(high, HALO), mid[rows - 1 : rows])
            return jnp.concatenate([first, mid, last], axis=0)

        plane = full(0)
        coef[e] = plane
        src[e] = full(2)
        face_y[e] = face(plane, pltpu.roll(plane, ext_y - 1, 0))
        face_z[e] = jnp.where(lane_index == zsize - 1, plane, face(plane, pltpu.roll(plane, zsize - 1, 1)))
        before = jnp.maximum(e - 1, 0)
        face_x[before] = face(coef[before], plane)

    def x_inside(e):
        return ((e >= HALO) | has_xlo) & ((e < ext_x - HALO) | has_xhi)

    def masked(e, value):
        return jnp.where(y_inside & x_inside(e), value, 0.0)

    def taps_of(ref, y0, n):
        return jnp.concatenate([ref[s, y0 : y0 + n].reshape(n * taps, lanes) for s in range(2)], axis=1)

    def convolve(e, k):
        result = jnp.dot(
            weights_fwd[...], taps_of(fwide.at[e], STRIP * k, STRIP + 2), preferred_element_type=F32
        )
        start = (1 + STRIP * k) * channels
        pre_ref[jnp.maximum(e - 2, 0), start : start + strip] = conv_b[k] + result[2 * strip :]
        conv_b[k] = conv_a[k] + result[strip : 2 * strip]
        conv_a[k] = result[:strip]

    def activate(px, yb):
        pre = pre_ref[px, yb * block : (yb + 1) * block]
        active = pre * sigmoid(pre)
        sums = jnp.sum((active * proj_block).reshape(8, channels, zsize), axis=1)
        inside = y_inside[8 * yb : 8 * yb + 8] & x_inside(px + 1)
        vfield[px, 8 * yb : 8 * yb + 8, :] = jnp.where(inside, sums, 0.0)

    for k in range(yblocks):
        fill_cells(0, k)
    fill_fields(0)

    def conv_step(e, carry):
        for k in range(strips):
            convolve(e - 1, k)
            for m in range(yblocks):
                if m * strips // yblocks == k:
                    activate(jnp.maximum(e - 4, 0), m)
                    fill_cells(e, m)
        fill_fields(e)
        return carry

    lax.fori_loop(1, ext_x, conv_step, 0)
    for k in range(strips):
        convolve(ext_x - 1, k)
    for k in range(yblocks):
        activate(ext_x - 4, k)
    for k in range(yblocks):
        activate(ext_x - 3, k)

    @pl.when(jnp.logical_not(has_xlo))
    def _():
        face_x[HALO - 1] = coef[HALO]

    @pl.when(jnp.logical_not(has_xhi))
    def _():
        face_x[ext_x - HALO - 1] = coef[ext_x - HALO - 1]

    def operator(e, below, centre, above):
        flux_y = face_y[e] * (centre - pltpu.roll(centre, ext_y - 1, 0))
        next_z = jnp.where(lane_index == zsize - 1, 0.0, pltpu.roll(centre, zsize - 1, 1))
        flux_z = face_z[e] * (centre - next_z)
        left_z = jnp.where(lane_index == 0, -coef[e] * centre, pltpu.roll(flux_z, 1, 1))
        total = face_x[e] * (centre - above) + face_x[e - 1] * (centre - below)
        return total + (flux_y - pltpu.roll(flux_y, 1, 0)) + (flux_z - left_z)

    def residual_step(i, carry):
        value = operator(i + 2, vfield[i], vfield[i + 1], vfield[i + 2]) - src[i + 2]
        rfield[i] = masked(i + 2, value)
        return carry

    lax.fori_loop(0, ext_x - 4, residual_step, 0, unroll=4)

    def adjoint_step(i, carry):
        afield[i] = masked(i + 3, operator(i + 3, rfield[i], rfield[i + 1], rfield[i + 2]))
        return carry

    lax.fori_loop(0, ext_x - 6, adjoint_step, 0, unroll=5)

    def residual_out(x, carry):
        value = rfield[x + 2][HALO : HALO + rows]
        low = value[:, :lanes]
        high = value[:, lanes:]
        res_own[x] = jnp.where(half == 0, low, high)
        res_send[x] = jnp.where(half == 0, high, low)
        return carry

    lax.fori_loop(0, inner, residual_out, 0, unroll=4)

    def grad_block(i, yb, slot):
        pre = pre_ref[i + 2, yb * block : (yb + 1) * block]
        sig = sigmoid(pre)
        near_adj = afield[i, 8 * yb : 8 * yb + 8, :]
        adj = jnp.broadcast_to(near_adj[:, None, :], (8, channels, zsize)).reshape(block, zsize)
        slope = sig * (1.0 + pre * (1.0 - sig))
        spread(slot, (adj * proj_block * slope).astype(BF16), 8 * yb)
        lo = max(HALO - 8 * yb, 0)
        hi = min(HALO + rows - 8 * yb, 8)
        term = (adj * (pre * sig))[lo * channels : hi * channels]
        total = term[:channels]
        for y in range(1, hi - lo):
            total = total + term[y * channels : (y + 1) * channels]
        pacc[...] += jnp.where((i >= 1) & (i <= inner), total, 0.0)

    def back_product(b, slot, weights):
        return jnp.dot(weights, taps_of(slot, HALO - 1 + 8 * b, 10), preferred_element_type=F32)

    def store_plane(x, parts):
        value = jnp.concatenate([p.reshape(channels, 8, zsize) for p in parts], axis=1).astype(BF16)
        low = value[:, :, :lanes]
        high = value[:, :, lanes:]
        fg_own[:, x] = jnp.where(half == 0, low, high)
        fg_send[:, x] = jnp.where(half == 0, high, low)

    def multiply(i, slot, make):
        parts = []
        centres = []
        for b in range(oblocks):
            y0 = HALO + 8 * b
            pieces = [slot[s, y0 : y0 + 8, channels : 2 * channels, :].reshape(block, lanes) for s in range(2)]
            centres.append(jnp.concatenate(pieces, axis=1))
        for k in range(max(3, oblocks, yblocks)):
            if k < oblocks:
                result = back_product(k, slot, weights_bwd[...])
                parts.append(acc_b[k] + result[2 * block :])
                acc_b[k] = acc_a[k] + result[block : 2 * block]
                acc_a[k] = result[:block]
            if k < 3:
                total = kacc[k]
                for b in range(oblocks):
                    total = total + lax.dot_general(
                        taps_of(fwide.at[i + HALO - 2 + k], HALO - 1 + 8 * b, 10),
                        centres[b],
                        (((1,), (1,)), ((), ())),
                        preferred_element_type=F32,
                    )
                kacc[k] = total
            if k < yblocks:
                make(k)
        store_plane(jnp.maximum(i - 2, 0), parts)

    for k in range(yblocks):
        grad_block(0, k, slot_a)
    for b in range(oblocks):
        acc_a[b] = back_product(b, slot_a, weights_bwd[:block])
        acc_b[b] = jnp.zeros((block, zsize), F32)
    for k in range(yblocks):
        grad_block(1, k, slot_b)

    def grad_step(t, carry):
        odd = 2 * t - 1
        multiply(odd, slot_b, lambda k: grad_block(odd + 1, k, slot_a))
        multiply(odd + 1, slot_a, lambda k: grad_block(odd + 2, k, slot_b))
        return carry

    lax.fori_loop(1, inner // 2 + 1, grad_step, 0)
    store_plane(inner - 1, [acc_b[b] + back_product(b, slot_b, weights_bwd[2 * block :]) for b in range(oblocks)])

    lane_group = lax.broadcasted_iota(jnp.int32, (3 * taps, block), 1) // channels
    sub_row = lax.broadcasted_iota(jnp.int32, (3 * taps, block), 0) % (block // channels)
    per_dx = 3 * taps * channels // block
    for dx in range(3):
        picked = jnp.zeros((3 * taps, block), F32)
        for y in range(8):
            picked = jnp.where(lane_group == y, kacc[dx, y * taps : y * taps + 3 * taps], picked)
        step = channels
        while step < block:
            picked = picked + pltpu.roll(picked, step, 1)
            step *= 2
        packed = jnp.where(lane_group == sub_row, picked, 0.0).reshape(per_dx, block // channels, block)
        grads[dx * per_dx : (dx + 1) * per_dx, :] = jnp.sum(packed, axis=1)
    per_channel = jnp.sum(pacc[...], axis=1, keepdims=True)
    chan_row = lax.broadcasted_iota(jnp.int32, (channels, block), 0)
    chan_lane = lax.broadcasted_iota(jnp.int32, (channels, block), 1)
    flat = jnp.sum(jnp.where(chan_row == chan_lane, per_channel, 0.0), axis=0, keepdims=True)
    grads[3 * per_dx :, :] = jnp.broadcast_to(flat, (grads.shape[0] - 3 * per_dx, block))


def main(channels, rows, proj, weights, tensors, edges):
    own, swap = tensors[0], tensors[1]
    sides = len(edges) // 4
    lanes = own.shape[2]
    zsize = 2 * lanes
    wide = swap.shape[0]
    ext_x = wide + HALO
    ext_y = rows + 2 * HALO
    inner = ext_x - 2 * HALO
    taps = 3 * channels
    block = 8 * channels
    yblocks = ext_y // 8
    grad_rows = 27 * channels * channels // block
    out_rows = -(-(grad_rows + 1) // 8) * 8
    vmem = pl.BlockSpec(memory_space=pltpu.VMEM)
    plane = (ext_y, zsize)
    slot = pltpu.VMEM((2, ext_y, taps, lanes), BF16)
    strip = pltpu.VMEM(((ext_y - 2) // STRIP, STRIP * channels, zsize), F32)
    return pl.pallas_call(
        lambda *refs: main_kernel(channels, rows, sides, *refs),
        out_shape=[
            jax.ShapeDtypeStruct((inner, rows, lanes), F32),
            jax.ShapeDtypeStruct((inner, rows, lanes), F32),
            jax.ShapeDtypeStruct((channels, inner, rows, lanes), BF16),
            jax.ShapeDtypeStruct((channels, inner, rows, lanes), BF16),
            jax.ShapeDtypeStruct((out_rows, block), F32),
        ],
        in_specs=[pl.BlockSpec(memory_space=pltpu.SMEM)] + [vmem] * (2 + len(tensors) + len(edges)),
        out_specs=[vmem] * 5,
        scratch_shapes=[
            pltpu.VMEM((ext_x, 2, ext_y, taps, lanes), BF16),
            slot,
            slot,
            pltpu.VMEM((ext_x - 2, ext_y * channels, zsize), F32),
            pltpu.VMEM((ext_x,) + plane, F32),
            pltpu.VMEM((ext_x,) + plane, F32),
            pltpu.VMEM((ext_x - 2,) + plane, F32),
            pltpu.VMEM((ext_x,) + plane, F32),
            pltpu.VMEM((ext_x,) + plane, F32),
            pltpu.VMEM((ext_x,) + plane, F32),
            pltpu.VMEM((ext_x - 4,) + plane, F32),
            pltpu.VMEM((ext_x - 6,) + plane, F32),
            strip,
            strip,
            pltpu.VMEM((rows // 8, block, zsize), F32),
            pltpu.VMEM((rows // 8, block, zsize), F32),
            pltpu.VMEM((3, 10 * taps, block), F32),
            pltpu.VMEM((channels, zsize), F32),
        ],
        compiler_params=pltpu.CompilerParams(vmem_limit_bytes=40 * 1024 * 1024),
        name="step",
    )(proj, *weights, *tensors, *edges)


def local(feats, kernel, proj, perm, source):
    channels, planes, rows, lanes = feats.shape
    sizes = tuple(lax.axis_size(a) for a in GROUP)
    ny = sizes[1]
    half = lax.axis_index("gz")
    sides = 1 if ny == 2 else 2

    def send(value, target):
        return lax.ppermute(value, GROUP, routes(sizes, target))

    def partner(value):
        return send(value, lambda x, y, z: (x, y, 1 - z))

    def to_near(value):
        return send(value, lambda x, y, z: (x + 1 if z == 0 else x - 1, y, z))

    def to_far(value):
        return send(value, lambda x, y, z: (x - 1 if z == 0 else x + 1, y, 1 - z))

    own, swap, near, far, *edges = pack(feats, perm, source, sides)
    received = []
    for side in range(sides):

        def step_y(y, side=side):
            if sides == 1:
                return 1 - y
            return y + 1 if side == 0 else y - 1

        received.append(send(edges[side], lambda x, y, z: (x, step_y(y), z)))
    swapped = partner(swap)
    *received, swapped = lax.optimization_barrier((*received, swapped))
    tensors = [own, swapped, to_near(near), to_far(far)]
    wide = planes - HALO
    got = []
    for value in received:
        got += [
            value,
            partner(value),
            to_near(lax.dynamic_slice_in_dim(value, wide * (1 - half), HALO, 0)),
            to_far(lax.dynamic_slice_in_dim(value, wide * half, HALO, 0)),
        ]
    weights = banded_weights(kernel)
    res_own, res_send, fg_own, fg_send, grads = main(channels, rows, proj, weights, tensors, got)

    res_got = partner(res_send)
    fg_got = partner(fg_send)

    def ordered(mine, other, axis):
        return jnp.where(
            half == 0, jnp.concatenate([mine, other], axis), jnp.concatenate([other, mine], axis)
        )

    residual = ordered(res_own, res_got, 0)
    feats_grad = ordered(fg_own, fg_got, 1)
    grads = grads + partner(grads)
    for axis in ("gy", "gx"):
        count = lax.axis_size(axis)
        step = 1
        while step < count:
            grads = grads + lax.ppermute(grads, axis, [(i, i ^ step) for i in range(count)])
            step *= 2
    grad_rows = 27 * channels * channels // grads.shape[1]
    kernel_grad = grads[:grad_rows].reshape(27, channels, channels).transpose(0, 2, 1)
    proj_grad = grads[grad_rows, :channels]
    return (residual, kernel_grad, proj_grad, feats_grad)


def solution(mesh):
    in_specs = (
        P(None, ("grp", "gx"), "gy", "gz"),
        P(),
        P(),
        P(("grp", "gx"), "gy", "gz"),
        P(("grp", "gx"), "gy", "gz"),
    )
    out_specs = (
        P(("grp", "gx"), "gy", "gz"),
        P("grp", None, None),
        P("grp"),
        P(None, ("grp", "gx"), "gy", "gz"),
    )
    return jax.shard_map(local, mesh=mesh, in_specs=in_specs, out_specs=out_specs, check_vma=False)
```
